256 devices in a mesh: seq: 64 (over x, z, core), tp: 4 (over y).
Axes of the slice: x: 4, y: 4, z: 8, core: 2. Of those that a mesh axis runs over, the one named last changes fastest.
Arguments:
- hidden_states: bfloat16 [16384, 3584], P('seq', 'tp'), may hold values from -6 to 6
- queries: bfloat16 [16384, 3584], P('seq', 'tp'), may hold values from -6 to 6
- key_weight: bfloat16 [3584, 512], P(None, 'tp'), may hold values from -0.09375 to 0.09375
- value_weight: bfloat16 [3584, 512], P(None, 'tp'), may hold values from -0.09375 to 0.09375
- output_weight: bfloat16 [3584, 3584], P('tp'), may hold values from -1.5 to 1.5
- prefix_keys: bfloat16 [16384, 512], P('seq', 'tp'), may hold values from -64 to 64
- prefix_values: bfloat16 [16384, 512], P('seq', 'tp'), may hold values from -6 to 6
- reads: int32 [64, 16], replicated, may hold values from 0 to 255, as said below
- out_grad: bfloat16 [16384, 3584], P('seq', 'tp'), may hold values from -6 to 6
Outputs:
- layer_output: bfloat16 [16384, 3584], P('seq', 'tp')
- prefix_key_grad: float32 [16384, 512], P('seq', 'tp')
- prefix_value_grad: float32 [16384, 512], P('seq', 'tp')
The draws below stay inside these ranges and needn't reach their ends.
Inputs may be any that keep to these rules, and one draw needn't show every extreme that they name: Entry l of a row is the row's node at depth l of a prefix tree, one of the blocks l * (16) to (l + 1) * 16 - 1; two rows that share a node share all its ancestors, and all rows share the root. Block b is held by index b // 4 of seq; every row names exactly 1 block of each index that it reads from.
All inputs are finite; a program needn't handle non-finite values.
Results may differ from the reference program's by a relative error of at most 0.0095.
Values may be sent and summed in bfloat16 or wider, within the bound.
A program may use at most 128 MiB of HBM per device.

```python
import jax
import jax.numpy as jnp
from jax import lax

D = 3584
QH = 28
KVH = 4
HD = 128
TOK_DEV = 256
PBLK = 64
READS = 16
NBLK = 256
TOKENS = 16384
N_SEQ = 64
N_TP = 4


def draw_reads(key, part):
    per_level = NBLK // READS
    log_width = per_level.bit_length() - 1
    order = jax.random.permutation(jax.random.fold_in(key, 11), N_SEQ).astype(jnp.int32)
    levels = jnp.arange(READS, dtype=jnp.int32)
    branch = (2 ** jnp.minimum(levels, log_width)).astype(jnp.int32)
    node = order[:, None] * branch[None, :] // N_SEQ
    slot_noise = jax.random.randint(jax.random.fold_in(key, 23), (READS, per_level), 0, 1024) * per_level + jnp.arange(per_level, dtype=jnp.int32)[None, :]
    slot_order = jnp.argsort(slot_noise, axis=1).astype(jnp.int32)
    chosen = slot_order[levels[None, :], node]
    return (levels[None, :] * per_level + chosen).astype(jnp.int32)


def draw_prefix_keys(key, part):
    row_total = NBLK * PBLK
    col_total = KVH * HD
    base_values = jax.random.normal(jax.random.fold_in(key, 3), (row_total, col_total), jnp.float32)
    return jnp.clip(base_values, -6.0, 6.0).astype(jnp.bfloat16)


def block_levels(rng, dims, shards, least, high):
    loudness, own = 1.0, jax.random.fold_in(rng, 6)
    for dim, shards_of in shards:
        steps = jnp.exp(jax.random.uniform(jax.random.fold_in(own, dim), (shards_of,), jnp.float32, least / len(shards), high / len(shards)))
        loudness = loudness * jnp.repeat(steps, dims[dim] // shards_of).reshape([-1 if axis == dim else 1 for axis in range(len(dims))])
    return loudness


def normal_values(stream_key, dims, spread, limit, cuts=(), kind=jnp.bfloat16):
    entries = spread * jax.random.normal(stream_key, dims, jnp.float32)
    if cuts:
        entries = entries * block_levels(stream_key, dims, cuts, -0.22, 0.18)
    return jnp.clip(entries, -limit, limit).astype(kind)


def setup_inputs(seed: int = 0) -> dict:
    key_list = jax.random.split(jax.random.key(seed), 10)
    return {
        "hidden_states": normal_values(key_list[0], (TOKENS, D), 1.0, 6.0, ((0, 64), (1, 4))),
        "queries": normal_values(key_list[1], (TOKENS, QH * HD), 1.0, 6.0, ((0, 64), (1, 4))),
        "key_weight": normal_values(key_list[2], (D, KVH * HD), D ** -0.5, 0.09375, ((1, 4),)),
        "value_weight": normal_values(key_list[3], (D, KVH * HD), D ** -0.5, 0.09375, ((1, 4),)),
        "output_weight": normal_values(key_list[4], (QH * HD, D), (max(1, QH * HD // 256)) ** -0.5, 1.5, ((0, 4),)),
        "prefix_keys": draw_prefix_keys(jax.random.fold_in(key_list[9], 71), 0),
        "prefix_values": normal_values(key_list[6], (NBLK * PBLK, KVH * HD), 1.0, 6.0, ((0, 64), (1, 4))),
        "reads": draw_reads(jax.random.fold_in(key_list[9], 71), 0),
        "out_grad": normal_values(key_list[8], (TOKENS, D), 1.0, 6.0, ((0, 64), (1, 4))),
    }


def attend_block(queries, keys_prefix, values_prefix, keys_own, values_own, head_grads, scaling):
    length = queries.shape[0]
    scores_prefix = jnp.einsum('tkgd,pkd->kgtp', queries, keys_prefix) * scaling
    scores_own = jnp.einsum('tkgd,ukd->kgtu', queries, keys_own) * scaling
    causal = jnp.arange(length)[None, :] <= jnp.arange(length)[:, None]
    masked_own = jnp.where(causal[None, None], scores_own, -jnp.inf)
    peak_score = jnp.maximum(jnp.max(scores_prefix, axis=-1), jnp.max(masked_own, axis=-1))[..., None]
    exps_prefix = jnp.exp(scores_prefix - peak_score)
    exps_own = jnp.exp(masked_own - peak_score)
    denominator = (jnp.sum(exps_prefix, axis=-1) + jnp.sum(exps_own, axis=-1))[..., None]
    softmax_prefix = exps_prefix / denominator
    softmax_own = exps_own / denominator
    weights_prefix = lax.optimization_barrier(softmax_prefix.astype(jnp.bfloat16)).astype(jnp.float32)
    weights_own = lax.optimization_barrier(softmax_own.astype(jnp.bfloat16)).astype(jnp.float32)
    context = jnp.einsum('kgtp,pkd->tkgd', weights_prefix, values_prefix)
    context = context + jnp.einsum('kgtu,ukd->tkgd', weights_own, values_own)
    context = context.astype(jnp.bfloat16)
    slope_prefix = jnp.einsum('tkgd,pkd->kgtp', head_grads, values_prefix)
    slope_own = jnp.einsum('tkgd,ukd->kgtu', head_grads, values_own)
    row_delta = jnp.sum(softmax_prefix * slope_prefix, axis=-1) + jnp.sum(softmax_own * slope_own, axis=-1)
    score_grad = (softmax_prefix * (slope_prefix - row_delta[..., None])).astype(jnp.bfloat16)
    score_grad = lax.optimization_barrier(score_grad).astype(jnp.float32)
    value_grad = jnp.einsum('kgtp,tkgd->pkd', weights_prefix, head_grads)
    key_grad = jnp.einsum('kgtp,tkgd->pkd', score_grad, queries) * scaling
    return context, key_grad, value_grad


def reference(hidden_states, queries, key_weight, value_weight, output_weight, prefix_keys, prefix_values, reads, out_grad):
    scaling = HD ** -0.5
    groups = QH // KVH
    new_keys = jnp.dot(hidden_states, key_weight, preferred_element_type=jnp.float32).astype(jnp.bfloat16)
    new_values = jnp.dot(hidden_states, value_weight, preferred_element_type=jnp.float32).astype(jnp.bfloat16)
    context_grad = jnp.dot(out_grad, output_weight.T, preferred_element_type=jnp.float32).astype(jnp.bfloat16)
    cache_keys = prefix_keys.reshape(NBLK, PBLK, KVH, HD)
    cache_values = prefix_values.reshape(NBLK, PBLK, KVH, HD)

    def block_step(totals, inputs):
        key_total, value_total = totals
        block_queries, block_keys, block_values, block_grads, block_reads = inputs
        keys_prefix = cache_keys[block_reads].reshape(READS * PBLK, KVH, HD).astype(jnp.float32)
        values_prefix = cache_values[block_reads].reshape(READS * PBLK, KVH, HD).astype(jnp.float32)
        context, key_grad, value_grad = attend_block(
            block_queries.astype(jnp.float32), keys_prefix, values_prefix,
            block_keys.astype(jnp.float32), block_values.astype(jnp.float32),
            block_grads.astype(jnp.float32), scaling)
        key_total = key_total.at[block_reads].add(key_grad.reshape(READS, PBLK, KVH, HD))
        value_total = value_total.at[block_reads].add(value_grad.reshape(READS, PBLK, KVH, HD))
        return (key_total, value_total), context.reshape(TOK_DEV, QH * HD)

    inputs = (queries.reshape(N_SEQ, TOK_DEV, KVH, groups, HD),
              new_keys.reshape(N_SEQ, TOK_DEV, KVH, HD),
              new_values.reshape(N_SEQ, TOK_DEV, KVH, HD),
              context_grad.reshape(N_SEQ, TOK_DEV, KVH, groups, HD),
              reads)
    zeros_grad = jnp.zeros((NBLK, PBLK, KVH, HD), jnp.float32)
    (key_total, value_total), context_all = lax.scan(block_step, (zeros_grad, zeros_grad), inputs)
    context_all = context_all.reshape(TOKENS, QH * HD)
    head_share = QH * HD // N_TP
    layer_output = jnp.zeros((TOKENS, D), jnp.float32)
    for share_index in range(N_TP):
        share_out = jnp.dot(context_all[:, share_index * head_share:(share_index + 1) * head_share],
                            output_weight[share_index * head_share:(share_index + 1) * head_share],
                            preferred_element_type=jnp.float32).astype(jnp.bfloat16)
        layer_output = layer_output + lax.optimization_barrier(share_out).astype(jnp.float32)
    return (layer_output.astype(jnp.bfloat16),
            key_total.reshape(NBLK * PBLK, KVH * HD),
            value_total.reshape(NBLK * PBLK, KVH * HD))
```

```python
import functools

import jax
import jax.numpy as jnp
from jax import lax
from jax.experimental import pallas as pl
from jax.experimental.pallas import tpu as pltpu
from jax.sharding import PartitionSpec as P

HD = 128
PBLK = 64
NX, NZ = 4, 8
TP = 4
HEADS = 7
TOK = 256
KEYS = 1024
ALL = KEYS + TOK
FEAT = 896
HALF = TOK // 2
SCALE = HD ** -0.5
LOG2E = 1.4426950408889634
BF = jnp.bfloat16
F32 = jnp.float32
MESH = pl.DeviceIdType.MESH


def dot(a, b):
    return jnp.dot(a, b, preferred_element_type=F32)


def dot_nt(a, b):
    return lax.dot_general(a, b, (((1,), (1,)), ((), ())), preferred_element_type=F32)


def kernel(
    reads, hid, queries, key_w, value_w, out_w, pkeys, pvalues, og,
    out, gk, gv,
    hs, gs, wkv, wo, qv, qt, grp, snd, kv, vt, hot, st, es, ctxt, ctx, inv, cgacc, cgt, cgn,
    dss, gsend, grecv, psend, precv, own_grad, rs_own, rs_fwd, rs_mid, rs_in,
    load_sem, ys_sem, yr_sem, g_send, g_recv, a_send, a_recv, b_send, b_recv, p_send, p_recv,
    r_send, r_recv,
):
    seq = lax.axis_index("seq")
    tp = lax.axis_index("tp")
    core = seq % 2
    zpos = (seq // 2) % NZ
    xpos = seq // (2 * NZ)
    member = seq % 4
    level = seq // 4
    right = (tp + 1) % TP
    left = (tp + TP - 1) % TP
    across = (tp + 2) % TP
    step = 2 * (zpos % 2) - 1

    def seq_of(x, z):
        return (x * NZ + z) * 2 + core

    def reader(r):
        i, j = r // 4, r % 4
        return seq_of((xpos + i) % NX, (zpos + step * j + NZ) % NZ)

    def server(r):
        i, j = r // 4, r % 4
        even = (zpos + j) % 2
        z = (zpos + j - 2 * j * even + NZ) % NZ
        return seq_of((xpos + NX - i) % NX, z)

    def peer(p):
        low = member
        bit0, bit1 = low % 2, low // 2
        if p % 2:
            bit0 = 1 - bit0
        if p // 2:
            bit1 = 1 - bit1
        return bit1 * 2 + bit0

    barrier = pltpu.get_barrier_semaphore()
    for t in (left, right):
        pl.semaphore_signal(barrier, 1, device_id={"tp": t}, device_id_type=MESH)
    for p in (1, 2, 3):
        pl.semaphore_signal(
            barrier, 1, device_id={"seq": level * 4 + peer(p)}, device_id_type=MESH
        )
    for r in range(1, 16):
        pl.semaphore_signal(barrier, 1, device_id={"seq": reader(r)}, device_id_type=MESH)
        pl.semaphore_signal(barrier, 1, device_id={"seq": server(r)}, device_id_type=MESH)

    loads = []

    def load(src, dst):
        loads.append(pltpu.make_async_copy(src, dst, load_sem.at[len(loads)]))
        loads[-1].start()

    load(hid, hs.at[3])
    load(queries, qv)
    for j in range(TP):
        load(key_w.at[pl.ds(j * FEAT, FEAT)], wkv.at[j, :, pl.ds(0, HD)])
        load(value_w.at[pl.ds(j * FEAT, FEAT)], wkv.at[j, :, pl.ds(HD, HD)])
    load(og, gs.at[3])
    for j in range(TP):
        load(out_w.at[:, pl.ds(j * FEAT, FEAT)], wo.at[j])

    for b in range(4):
        grp[member * 4 + b, :, 0:HD] = pkeys[b * PBLK : (b + 1) * PBLK, :]
        grp[member * 4 + b, :, HD:] = pvalues[b * PBLK : (b + 1) * PBLK, :]

    pl.semaphore_wait(barrier, 35)

    def ring(src, dst, k):
        lo, hi = pl.ds(0, HALF), pl.ds(HALF, HALF)

        def copy(s, d, n, to):
            return pltpu.make_async_remote_copy(
                s, d, ys_sem.at[k + n], yr_sem.at[k + n],
                device_id={"tp": to}, device_id_type=MESH,
            )

        own = [
            copy(src.at[lo], dst.at[0, lo], 0, right),
            copy(src.at[hi], dst.at[1, hi], 1, left),
            copy(src.at[hi], dst.at[0, hi], 2, right),
            copy(src.at[lo], dst.at[1, lo], 3, left),
        ]
        forward = [
            copy(dst.at[0, lo], dst.at[2, lo], 4, right),
            copy(dst.at[1, hi], dst.at[2, hi], 5, left),
        ]
        return own, forward

    h_own, h_fwd = ring(hid, hs, 0)
    o_own, o_fwd = ring(og, gs, 6)
    for c in h_own:
        c.start()

    group = []
    for p in (3, 2, 1):
        c = pltpu.make_async_remote_copy(
            grp.at[pl.ds(member * 4, 4)], grp.at[pl.ds(member * 4, 4)],
            g_send.at[p], g_recv.at[p],
            device_id={"seq": level * 4 + peer(p)}, device_id_type=MESH,
        )
        c.start()
        group.append(c)

    rd = [lax.bitwise_and(reads[reader(r), level], 15) for r in range(16)]
    lane = lax.broadcasted_iota(jnp.int32, (TOK, 128), 1)
    sub = lax.broadcasted_iota(jnp.int32, (TOK, 128), 0)
    for h in range(8):
        want = jnp.where(lane < PBLK, rd[2 * h] * PBLK + lane, rd[2 * h + 1] * PBLK + lane - PBLK)
        for p in range(4):
            match = (sub + peer(p) * TOK) == want
            hot[p, :, h * 128 : (h + 1) * 128] = jnp.where(match, 1.0, 0.0).astype(BF)

    loads[1].wait()
    for h in range(HEADS):
        qt[h] = qv[:, h * HD : (h + 1) * HD].T

    h_own[0].wait_recv()
    h_fwd[0].start()
    h_own[1].wait_recv()
    h_fwd[1].start()

    for c in group:
        c.wait_recv()
    serve = [None]
    kv[0:PBLK, :] = grp[rd[0]]
    for r in range(1, 16):
        snd[r] = grp[rd[r]]
        c = pltpu.make_async_remote_copy(
            snd.at[r], kv.at[pl.ds(r * PBLK, PBLK)], a_send.at[r], a_recv.at[r],
            device_id={"seq": reader(r)}, device_id_type=MESH,
        )
        c.start()
        serve.append(c)

    loads[0].wait()
    for n in range(2, 10):
        loads[n].wait()
    total = dot(hs[3], wkv[tp])
    h_own[2].wait_recv()
    total += dot(hs[0], wkv[left])
    h_own[3].wait_recv()
    total += dot(hs[1], wkv[right])
    for c in o_own:
        c.start()
    h_fwd[0].wait_recv()
    h_fwd[1].wait_recv()
    total += dot(hs[2], wkv[across])
    kv[KEYS:ALL, :] = total.astype(BF)

    for r in range(1, 16):
        serve[r].wait_recv()
    vt[...] = kv[:, HD:].T

    key_pos = lax.broadcasted_iota(jnp.int32, (TOK, TOK), 0)
    tok_pos = lax.broadcasted_iota(jnp.int32, (TOK, TOK), 1)

    def forward(h, _):
        q_h = qt[h]
        peak = None
        for c in range(5):
            s = dot(kv[c * TOK : (c + 1) * TOK, 0:HD], q_h)
            if c == 4:
                s = jnp.where(key_pos <= tok_pos, s, -jnp.inf)
            st[c] = s
            top = jnp.max(s, axis=0, keepdims=True)
            peak = top if peak is None else jnp.maximum(peak, top)
        low = None
        for c in range(5):
            e = jnp.exp2((st[c] - peak) * (SCALE * LOG2E))
            part = jnp.sum(e, axis=0, keepdims=True)
            low = part if low is None else low + part
            es[h, c * TOK : (c + 1) * TOK, :] = e.astype(BF)
        scale = 1.0 / low
        inv[h] = jnp.broadcast_to(scale, (8, TOK))
        ctxt[h] = dot(vt[...], es[h]) * scale
        return 0

    lax.fori_loop(0, 4, forward, 0)
    o_own[0].wait_recv()
    o_fwd[0].start()
    o_own[1].wait_recv()
    o_fwd[1].start()
    lax.fori_loop(4, HEADS, forward, 0)
    for h in range(HEADS):
        ctx[:, h * HD : (h + 1) * HD] = ctxt[h].astype(BF).T

    for n in range(11, 15):
        loads[n].wait()

    def rs(src, dst, n, to):
        return pltpu.make_async_remote_copy(
            src, dst, r_send.at[n], r_recv.at[n], device_id={"tp": to}, device_id_type=MESH
        )

    lo, hi = pl.ds(0, HALF), pl.ds(HALF, HALF)
    rs_far = [
        rs(rs_fwd.at[lo], rs_mid.at[0], 0, right),
        rs(rs_fwd.at[hi], rs_mid.at[1], 1, left),
    ]
    rs_now = [
        rs(rs_own.at[0, hi], rs_in.at[0, hi], 2, right),
        rs(rs_own.at[1, lo], rs_in.at[1, lo], 3, left),
    ]
    rs_late = [
        rs(rs_own.at[0, lo], rs_in.at[0, lo], 4, right),
        rs(rs_own.at[1, hi], rs_in.at[1, hi], 5, left),
    ]
    rs_fwd[...] = dot(ctx[...], wo[across]).astype(BF)
    for c in rs_far:
        c.start()
    rs_own[0] = dot(ctx[...], wo[right]).astype(BF)
    rs_own[1] = dot(ctx[...], wo[left]).astype(BF)
    for c in rs_now:
        c.start()

    loads[10].wait()
    cgacc[...] = dot_nt(wo[tp], gs[3])
    o_own[2].wait_recv()
    cgacc[...] += dot_nt(wo[left], gs[0])
    o_own[3].wait_recv()
    cgacc[...] += dot_nt(wo[right], gs[1])
    o_fwd[0].wait_recv()
    o_fwd[1].wait_recv()
    cgacc[...] += dot_nt(wo[across], gs[2])
    for h in range(HEADS):
        scaled = (cgacc[h * HD : (h + 1) * HD, :] * inv[h, 0:1, :]).astype(BF)
        cgt[h] = scaled
        cgn[h] = scaled.T
        delta = jnp.sum(scaled.astype(F32) * ctxt[h], axis=0, keepdims=True)
        inv[h] = jnp.broadcast_to(delta, (8, TOK))

    back = [None] * 16

    def backward(i):
        rows = slice(i * TOK, (i + 1) * TOK)
        vals = kv[rows, HD:]
        dk = None
        for h in range(HEADS):
            slope = dot(vals, cgt[h])
            e = es[h, rows, :]
            grad = (e.astype(F32) * (slope - inv[h, 0:1, :])).astype(BF)
            dk_h = dot(grad, qv[:, h * HD : (h + 1) * HD])
            dv_h = dot(e, cgn[h])
            dk = dk_h if dk is None else dk + dk_h
            dv = dv_h if h == 0 else dv + dv_h
        gsend[rows, 0:HD] = dk.astype(BF)
        gsend[rows, HD:] = dv.astype(BF)
        for j in range(4):
            r = i * 4 + j
            if r == 0:
                grecv[0:PBLK, :] = gsend[0:PBLK, :]
                continue
            place = pl.ds(r * PBLK, PBLK)
            c = pltpu.make_async_remote_copy(
                gsend.at[place], grecv.at[place], b_send.at[r], b_recv.at[r],
                device_id={"seq": server(r)}, device_id_type=MESH,
            )
            c.start()
            back[r] = c

    backward(2)
    backward(1)
    rs_far[0].wait_recv()
    rs_own[0, 0:HALF] = (rs_own[0, 0:HALF].astype(F32) + rs_mid[0].astype(F32)).astype(BF)
    rs_late[0].start()
    rs_far[1].wait_recv()
    rs_own[1, HALF:] = (rs_own[1, HALF:].astype(F32) + rs_mid[1].astype(F32)).astype(BF)
    rs_late[1].start()
    backward(3)
    backward(0)

    mine = dot(ctx[...], wo[tp])

    for r in range(1, 16):
        back[r].wait_recv()
    spread = []
    for p in (3, 2, 1):
        psend[p] = dot(hot[p], grecv[...]).astype(BF)
        c = pltpu.make_async_remote_copy(
            psend.at[p], precv.at[p], p_send.at[p], p_recv.at[p],
            device_id={"seq": level * 4 + peer(p)}, device_id_type=MESH,
        )
        c.start()
        spread.append(c)
    own_grad[...] = dot(hot[0], grecv[...])

    for c in rs_now + rs_late:
        c.wait_recv()
    out[...] = (mine + rs_in[0].astype(F32) + rs_in[1].astype(F32)).astype(BF)

    for c in spread:
        c.wait_recv()
    total = own_grad[...] + precv[1].astype(F32) + precv[2].astype(F32) + precv[3].astype(F32)
    gk[...] = total[:, 0:HD] * SCALE
    gv[...] = total[:, HD:]

    for c in h_own + h_fwd + o_own + o_fwd + group + rs_far + rs_now + rs_late + spread:
        c.wait_send()
    for r in range(1, 16):
        serve[r].wait_send()
        back[r].wait_send()


def local(*args):
    hidden, queries, key_w, value_w, out_w, pkeys, pvalues, reads, og = args
    vmem = pl.BlockSpec(memory_space=pltpu.VMEM)
    hbm = pl.BlockSpec(memory_space=pl.ANY)
    dma = pltpu.SemaphoreType.DMA
    V = pltpu.VMEM
    return pl.pallas_call(
        kernel,
        out_shape=(
            jax.ShapeDtypeStruct((TOK, FEAT), BF),
            jax.ShapeDtypeStruct((TOK, HD), F32),
            jax.ShapeDtypeStruct((TOK, HD), F32),
        ),
        in_specs=[pl.BlockSpec(memory_space=pltpu.SMEM), hbm, hbm, hbm, hbm, hbm, vmem, vmem, hbm],
        out_specs=(vmem, vmem, vmem),
        scratch_shapes=[
            V((4, TOK, FEAT), BF),
            V((4, TOK, FEAT), BF),
            V((TP, FEAT, 2 * HD), BF),
            V((TP, FEAT, FEAT), BF),
            V((TOK, FEAT), BF),
            V((HEADS, HD, TOK), BF),
            V((16, PBLK, 2 * HD), BF),
            V((16, PBLK, 2 * HD), BF),
            V((ALL, 2 * HD), BF),
            V((HD, ALL), BF),
            V((4, TOK, KEYS), BF),
            V((5, TOK, TOK), F32),
            V((HEADS, ALL, TOK), BF),
            V((HEADS, HD, TOK), F32),
            V((TOK, FEAT), BF),
            V((HEADS, 8, TOK), F32),
            V((FEAT, TOK), F32),
            V((HEADS, HD, TOK), BF),
            V((HEADS, TOK, HD), BF),
            V((8, 128), F32),
            V((KEYS, 2 * HD), BF),
            V((KEYS, 2 * HD), BF),
            V((4, TOK, 2 * HD), BF),
            V((4, TOK, 2 * HD), BF),
            V((TOK, 2 * HD), F32),
            V((2, TOK, FEAT), BF),
            V((TOK, FEAT), BF),
            V((2, HALF, FEAT), BF),
            V((2, TOK, FEAT), BF),
            dma((15,)), dma((12,)), dma((12,)), dma((4,)), dma((4,)), dma((16,)), dma((16,)),
            dma((16,)), dma((16,)), dma((4,)), dma((4,)), dma((6,)), dma((6,)),
        ],
        compiler_params=pltpu.CompilerParams(
            collective_id=0, has_side_effects=True, vmem_limit_bytes=56 * 1024 * 1024
        ),
    )(reads, hidden, queries, key_w, value_w, out_w, pkeys, pvalues, og)


def solution(mesh):
    in_specs = (
        P("seq", "tp"), P("seq", "tp"), P(None, "tp"), P(None, "tp"), P("tp", None),
        P("seq", "tp"), P("seq", "tp"), P(), P("seq", "tp"),
    )
    out_specs = (P("seq", "tp"), P("seq", "tp"), P("seq", "tp"))
    return jax.shard_map(local, mesh=mesh, in_specs=in_specs, out_specs=out_specs, check_vma=False)
```

```python
import functools

import jax
import jax.numpy as jnp
from jax import lax
from jax.experimental import pallas as pl
from jax.experimental.pallas import tpu as pltpu
from jax.sharding import PartitionSpec as P

HD = 128
PBLK = 64
NX, NZ = 4, 8
TP = 4
HEADS = 7
TOK = 256
KEYS = 1024
ALL = KEYS + TOK
FEAT = 896
HALF = TOK // 2
SCALE = HD ** -0.5
LOG2E = 1.4426950408889634
BF = jnp.bfloat16
F32 = jnp.float32
MESH = pl.DeviceIdType.MESH


def dot(a, b):
    return jnp.dot(a, b, preferred_element_type=F32)


def dot_nt(a, b):
    return lax.dot_general(a, b, (((1,), (1,)), ((), ())), preferred_element_type=F32)


def kernel(
    reads_hbm, hid, queries, key_w, value_w, out_w, pkeys, pvalues, og,
    out, grads,
    reads, hs, gs, wkv, wo, qv, qt, grp, snd, kv, vt, hot, st, es, ctxt, ctx, inv, cgacc, cgt, cgn,
    gsend, grecv, psend, precv, own_grad, rs_own, rs_fwd, rs_mid, rs_in,
    load_sem, ys_sem, yr_sem, g_send, g_recv, a_send, a_recv, b_send, b_recv, p_send, p_recv,
    r_send, r_recv,
):
    seq = lax.axis_index("seq")
    tp = lax.axis_index("tp")
    core = seq % 2
    zpos = (seq // 2) % NZ
    xpos = seq // (2 * NZ)
    member = seq % 4
    level = seq // 4
    right = (tp + 1) % TP
    left = (tp + TP - 1) % TP
    across = (tp + 2) % TP
    step = 2 * (zpos % 2) - 1

    def seq_of(x, z):
        return (x * NZ + z) * 2 + core

    def reader(r):
        i, j = r // 4, r % 4
        return seq_of((xpos + i) % NX, (zpos + step * j + NZ) % NZ)

    def server(r):
        i, j = r // 4, r % 4
        even = (zpos + j) % 2
        z = (zpos + j - 2 * j * even + NZ) % NZ
        return seq_of((xpos + NX - i) % NX, z)

    def peer(p):
        low = member
        bit0, bit1 = low % 2, low // 2
        if p % 2:
            bit0 = 1 - bit0
        if p // 2:
            bit1 = 1 - bit1
        return bit1 * 2 + bit0

    barrier = pltpu.get_barrier_semaphore()
    for t in (left, right):
        pl.semaphore_signal(barrier, 1, device_id={"tp": t}, device_id_type=MESH)
    for p in (1, 2, 3):
        pl.semaphore_signal(
            barrier, 1, device_id={"seq": level * 4 + peer(p)}, device_id_type=MESH
        )
    for r in range(1, 16):
        pl.semaphore_signal(barrier, 1, device_id={"seq": server(r)}, device_id_type=MESH)

    loads = []

    def load(src, dst):
        loads.append(pltpu.make_async_copy(src, dst, load_sem.at[len(loads)]))
        loads[-1].start()

    mine = grp.at[pl.ds(member * 4, 4)]
    first = [pltpu.make_async_copy(reads_hbm, reads, load_sem.at[23])]
    for b in range(4):
        rows = pl.ds(b * PBLK, PBLK)
        for n, (src, col) in enumerate(((pkeys, 0), (pvalues, HD))):
            first.append(
                pltpu.make_async_copy(
                    src.at[rows], grp.at[member * 4 + b, :, pl.ds(col, HD)],
                    load_sem.at[15 + 2 * b + n],
                )
            )
    for c in first:
        c.start()
    load(hid, hs.at[3])
    load(queries, qv)
    for j in range(TP):
        load(key_w.at[pl.ds(j * FEAT, FEAT)], wkv.at[j, :, pl.ds(0, HD)])
        load(value_w.at[pl.ds(j * FEAT, FEAT)], wkv.at[j, :, pl.ds(HD, HD)])
    load(og, gs.at[3])
    for j in range(TP):
        load(out_w.at[:, pl.ds(j * FEAT, FEAT)], wo.at[j])

    for c in first:
        c.wait()

    pl.semaphore_wait(barrier, 20)

    def ring(src, dst, k):
        lo, hi = pl.ds(0, HALF), pl.ds(HALF, HALF)

        def copy(s, d, n, to):
            return pltpu.make_async_remote_copy(
                s, d, ys_sem.at[k + n], yr_sem.at[k + n],
                device_id={"tp": to}, device_id_type=MESH,
            )

        own = [
            copy(src.at[lo], dst.at[0, lo], 0, right),
            copy(src.at[hi], dst.at[1, hi], 1, left),
            copy(src.at[hi], dst.at[0, hi], 2, right),
            copy(src.at[lo], dst.at[1, lo], 3, left),
        ]
        forward = [
            copy(dst.at[0, lo], dst.at[2, lo], 4, right),
            copy(dst.at[1, hi], dst.at[2, hi], 5, left),
        ]
        return own, forward

    h_own, h_fwd = ring(hid, hs, 0)
    o_own, o_fwd = ring(og, gs, 6)
    for c in h_own:
        c.start()

    group = []
    for p in (3, 2, 1):
        c = pltpu.make_async_remote_copy(
            mine, mine,
            g_send.at[p], g_recv.at[p],
            device_id={"seq": level * 4 + peer(p)}, device_id_type=MESH,
        )
        c.start()
        group.append(c)

    rd = [lax.bitwise_and(reads[level, reader(r)], 15) for r in range(16)]
    lane = lax.broadcasted_iota(jnp.int32, (TOK, 128), 1)
    sub = lax.broadcasted_iota(jnp.int32, (TOK, 128), 0)
    for h in range(8):
        want = jnp.where(lane < PBLK, rd[2 * h] * PBLK + lane, rd[2 * h + 1] * PBLK + lane - PBLK)
        for p in range(4):
            match = (sub + peer(p) * TOK) == want
            hot[p, :, h * 128 : (h + 1) * 128] = jnp.where(match, 1.0, 0.0).astype(BF)

    loads[1].wait()
    for h in range(HEADS):
        qt[h] = qv[:, h * HD : (h + 1) * HD].T

    h_own[0].wait_recv()
    h_fwd[0].start()
    h_own[1].wait_recv()
    h_fwd[1].start()

    for c in group:
        c.wait_recv()
    serve = [None]
    kv[0:PBLK, :] = grp[rd[0]]
    for r in range(1, 16):
        snd[r] = grp[rd[r]]
        c = pltpu.make_async_remote_copy(
            snd.at[r], kv.at[pl.ds(r * PBLK, PBLK)], a_send.at[r], a_recv.at[r],
            device_id={"seq": reader(r)}, device_id_type=MESH,
        )
        c.start()
        serve.append(c)

    loads[0].wait()
    for n in range(2, 10):
        loads[n].wait()
    total = dot(hs[3], wkv[tp])
    h_own[2].wait_recv()
    total += dot(hs[0], wkv[left])
    h_own[3].wait_recv()
    total += dot(hs[1], wkv[right])
    for c in o_own:
        c.start()
    h_fwd[0].wait_recv()
    h_fwd[1].wait_recv()
    total += dot(hs[2], wkv[across])
    kv[KEYS:ALL, :] = total.astype(BF)

    for r in range(1, 16):
        serve[r].wait_recv()
    vt[...] = kv[:, HD:].T

    key_pos = lax.broadcasted_iota(jnp.int32, (TOK, TOK), 0)
    tok_pos = lax.broadcasted_iota(jnp.int32, (TOK, TOK), 1)

    def forward(h, _):
        q_h = qt[h]
        peak = None
        for c in range(5):
            s = dot(kv[c * TOK : (c + 1) * TOK, 0:HD], q_h)
            if c == 4:
                s = jnp.where(key_pos <= tok_pos, s, -jnp.inf)
            st[c] = s
            top = jnp.max(s, axis=0, keepdims=True)
            peak = top if peak is None else jnp.maximum(peak, top)
        low = None
        for c in range(5):
            e = jnp.exp2((st[c] - peak) * (SCALE * LOG2E))
            part = jnp.sum(e, axis=0, keepdims=True)
            low = part if low is None else low + part
            es[h, c * TOK : (c + 1) * TOK, :] = e.astype(BF)
        scale = 1.0 / low
        inv[h] = jnp.broadcast_to(scale, (8, TOK))
        ctxt[h] = dot(vt[...], es[h]) * scale
        return 0

    lax.fori_loop(0, 4, forward, 0)
    o_own[0].wait_recv()
    o_fwd[0].start()
    o_own[1].wait_recv()
    o_fwd[1].start()
    lax.fori_loop(4, HEADS, forward, 0)
    for h in range(HEADS):
        ctx[:, h * HD : (h + 1) * HD] = ctxt[h].astype(BF).T

    for n in range(11, 15):
        loads[n].wait()

    def rs(src, dst, n, to):
        return pltpu.make_async_remote_copy(
            src, dst, r_send.at[n], r_recv.at[n], device_id={"tp": to}, device_id_type=MESH
        )

    lo, hi = pl.ds(0, HALF), pl.ds(HALF, HALF)
    rs_far = [
        rs(rs_fwd.at[lo], rs_mid.at[0], 0, right),
        rs(rs_fwd.at[hi], rs_mid.at[1], 1, left),
    ]
    rs_now = [
        rs(rs_own.at[0, hi], rs_in.at[0, hi], 2, right),
        rs(rs_own.at[1, lo], rs_in.at[1, lo], 3, left),
    ]
    rs_late = [
        rs(rs_own.at[0, lo], rs_in.at[0, lo], 4, right),
        rs(rs_own.at[1, hi], rs_in.at[1, hi], 5, left),
    ]
    rs_fwd[...] = dot(ctx[...], wo[across]).astype(BF)
    for c in rs_far:
        c.start()
    rs_own[0] = dot(ctx[...], wo[right]).astype(BF)
    rs_own[1] = dot(ctx[...], wo[left]).astype(BF)
    for c in rs_now:
        c.start()

    loads[10].wait()
    cgacc[...] = dot_nt(wo[tp], gs[3])
    o_own[2].wait_recv()
    cgacc[...] += dot_nt(wo[left], gs[0])
    o_own[3].wait_recv()
    cgacc[...] += dot_nt(wo[right], gs[1])
    o_fwd[0].wait_recv()
    o_fwd[1].wait_recv()
    cgacc[...] += dot_nt(wo[across], gs[2])
    for h in range(HEADS):
        scaled = (cgacc[h * HD : (h + 1) * HD, :] * inv[h, 0:1, :]).astype(BF)
        cgt[h] = scaled
        cgn[h] = scaled.T
        delta = jnp.sum(scaled.astype(F32) * ctxt[h], axis=0, keepdims=True)
        inv[h] = jnp.broadcast_to(delta, (8, TOK))

    back = [None] * 16

    def backward(i):
        rows = slice(i * TOK, (i + 1) * TOK)
        vals = kv[rows, HD:]
        dk = None
        for h in range(HEADS):
            slope = dot(vals, cgt[h])
            e = es[h, rows, :]
            grad = (e.astype(F32) * (slope - inv[h, 0:1, :])).astype(BF)
            dk_h = dot(grad, qv[:, h * HD : (h + 1) * HD])
            dv_h = dot(e, cgn[h])
            dk = dk_h if dk is None else dk + dk_h
            dv = dv_h if h == 0 else dv + dv_h
        gsend[rows, 0:HD] = dk.astype(BF)
        gsend[rows, HD:] = dv.astype(BF)
        for j in range(4):
            r = i * 4 + j
            if r == 0:
                grecv[0:PBLK, :] = gsend[0:PBLK, :]
                continue
            place = pl.ds(r * PBLK, PBLK)
            c = pltpu.make_async_remote_copy(
                gsend.at[place], grecv.at[place], b_send.at[r], b_recv.at[r],
                device_id={"seq": server(r)}, device_id_type=MESH,
            )
            c.start()
            back[r] = c

    backward(2)
    backward(1)
    rs_far[0].wait_recv()
    rs_own[0, 0:HALF] = (rs_own[0, 0:HALF].astype(F32) + rs_mid[0].astype(F32)).astype(BF)
    rs_late[0].start()
    rs_far[1].wait_recv()
    rs_own[1, HALF:] = (rs_own[1, HALF:].astype(F32) + rs_mid[1].astype(F32)).astype(BF)
    rs_late[1].start()
    backward(3)
    backward(0)

    kept = dot(ctx[...], wo[tp])

    for r in range(1, 16):
        back[r].wait_recv()
    spread = []
    for p in (3, 2, 1):
        psend[p] = dot(hot[p], grecv[...]).astype(BF)
        c = pltpu.make_async_remote_copy(
            psend.at[p], precv.at[p], p_send.at[p], p_recv.at[p],
            device_id={"seq": level * 4 + peer(p)}, device_id_type=MESH,
        )
        c.start()
        spread.append(c)
    own_grad[...] = dot(hot[0], grecv[...])

    for c in rs_now + rs_late:
        c.wait_recv()
    out[...] = (kept + rs_in[0].astype(F32) + rs_in[1].astype(F32)).astype(BF)

    for c in spread:
        c.wait_recv()
    total = own_grad[...] + precv[1].astype(F32) + precv[2].astype(F32) + precv[3].astype(F32)
    grads[:, 0:HD] = total[:, 0:HD] * SCALE
    grads[:, HD:] = total[:, HD:]

    for c in h_own + h_fwd + o_own + o_fwd + group + rs_far + rs_now + rs_late + spread:
        c.wait_send()
    for r in range(1, 16):
        serve[r].wait_send()
        back[r].wait_send()


def local(*args):
    hidden, queries, key_w, value_w, out_w, pkeys, pvalues, reads, og = args
    operands = (reads.T, hidden, queries, key_w, value_w, out_w, pkeys, pvalues, og)
    operands = [pltpu.with_memory_space_constraint(a, pltpu.HBM) for a in operands]
    vmem = pl.BlockSpec(memory_space=pltpu.VMEM)
    hbm = pl.BlockSpec(memory_space=pltpu.HBM)
    dma = pltpu.SemaphoreType.DMA
    V = pltpu.VMEM
    out, grads = pl.pallas_call(
        kernel,
        out_shape=(
            jax.ShapeDtypeStruct((TOK, FEAT), BF),
            jax.ShapeDtypeStruct((TOK, 2 * HD), F32),
        ),
        in_specs=[hbm] * 9,
        out_specs=(vmem, vmem),
        scratch_shapes=[
            pltpu.SMEM((16, 64), jnp.int32),
            V((4, TOK, FEAT), BF),
            V((4, TOK, FEAT), BF),
            V((TP, FEAT, 2 * HD), BF),
            V((TP, FEAT, FEAT), BF),
            V((TOK, FEAT), BF),
            V((HEADS, HD, TOK), BF),
            V((16, PBLK, 2 * HD), BF),
            V((16, PBLK, 2 * HD), BF),
            V((ALL, 2 * HD), BF),
            V((HD, ALL), BF),
            V((4, TOK, KEYS), BF),
            V((5, TOK, TOK), F32),
            V((HEADS, ALL, TOK), BF),
            V((HEADS, HD, TOK), F32),
            V((TOK, FEAT), BF),
            V((HEADS, 8, TOK), F32),
            V((FEAT, TOK), F32),
            V((HEADS, HD, TOK), BF),
            V((HEADS, TOK, HD), BF),
            V((KEYS, 2 * HD), BF),
            V((KEYS, 2 * HD), BF),
            V((4, TOK, 2 * HD), BF),
            V((4, TOK, 2 * HD), BF),
            V((TOK, 2 * HD), F32),
            V((2, TOK, FEAT), BF),
            V((TOK, FEAT), BF),
            V((2, HALF, FEAT), BF),
            V((2, TOK, FEAT), BF),
            dma((24,)), dma((12,)), dma((12,)), dma((4,)), dma((4,)), dma((16,)), dma((16,)),
            dma((16,)), dma((16,)), dma((4,)), dma((4,)), dma((6,)), dma((6,)),
        ],
        compiler_params=pltpu.CompilerParams(
            collective_id=0, has_side_effects=True, vmem_limit_bytes=40 * 1024 * 1024
        ),
    )(*operands)
    return out, grads[:, 0:HD], grads[:, HD:]


def solution(mesh):
    in_specs = (
        P("seq", "tp"), P("seq", "tp"), P(None, "tp"), P(None, "tp"), P("tp", None),
        P("seq", "tp"), P("seq", "tp"), P(), P("seq", "tp"),
    )
    out_specs = (P("seq", "tp"), P("seq", "tp"), P("seq", "tp"))
    return jax.shard_map(local, mesh=mesh, in_specs=in_specs, out_specs=out_specs, check_vma=False)
```

```python
import functools

import jax
import jax.numpy as jnp
from jax import lax
from jax.experimental import pallas as pl
from jax.experimental.pallas import tpu as pltpu
from jax.sharding import PartitionSpec as P

HD = 128
PBLK = 64
NX, NZ = 4, 8
TP = 4
HEADS = 7
TOK = 256
KEYS = 1024
FEAT = 896
HALF = TOK // 2
QUART = 4
QROWS = PBLK // QUART
PIECE = FEAT // (2 * NX)
SCALE = HD ** -0.5
LOG2E = 1.4426950408889634
BF = jnp.bfloat16
F32 = jnp.float32
MESH = pl.DeviceIdType.MESH
FAR_FIRST = (11, 10, 7, 15, 9, 8, 6, 14, 3, 2, 5, 13, 1, 4, 12)


def dot(a, b):
    return jnp.dot(a, b, preferred_element_type=F32)


def dot_nt(a, b):
    return lax.dot_general(a, b, (((1,), (1,)), ((), ())), preferred_element_type=F32)


def kernel(
    reads_hbm, hid, queries, key_w, value_w, out_w, pkeys, pvalues, og,
    out, grads,
    reads, hs, gs, wkv, wo, qv, qt, grp, snd, kv, vt, hot, st, es, peaks, lows, own_k, own_vt, new_own, ctxt, ctx, inv, cgacc, kvs, kvr, cgt, cgn,
    gsend, grecv, psend, precv, own_grad, rs_own, rs_fwd, rs_mid, rs_in,
    load_sem, ys_sem, yr_sem, g_send, g_recv, a_send, a_recv, b_send, b_recv, p_send, p_recv,
    r_send, r_recv, wy_send, wy_recv, wx_send, wx_recv, wc_send, wc_recv, kv_send, kv_recv,
):
    seq = lax.axis_index("seq")
    tp = lax.axis_index("tp")
    core = seq % 2
    zpos = (seq // 2) % NZ
    xpos = seq // (2 * NZ)
    member = seq % 4
    level = seq // 4
    right = (tp + 1) % TP
    left = (tp + TP - 1) % TP
    across = (tp + 2) % TP
    step = 2 * (zpos % 2) - 1

    def seq_of(x, z):
        return (x * NZ + z) * 2 + core

    def reader(r):
        i, j = r // 4, r % 4
        return seq_of((xpos + i) % NX, (zpos + step * j + NZ) % NZ)

    def server(r):
        i, j = r // 4, r % 4
        even = (zpos + j) % 2
        z = (zpos + j - 2 * j * even + NZ) % NZ
        return seq_of((xpos + NX - i) % NX, z)

    def peer(p):
        low = member
        bit0, bit1 = low % 2, low // 2
        if p % 2:
            bit0 = 1 - bit0
        if p // 2:
            bit1 = 1 - bit1
        return bit1 * 2 + bit0

    barrier = pltpu.get_barrier_semaphore()
    for t in (left, right, across):
        pl.semaphore_signal(barrier, 1, device_id={"tp": t}, device_id_type=MESH)
    for p in (1, 2, 3):
        pl.semaphore_signal(
            barrier, 1, device_id={"seq": level * 4 + peer(p)}, device_id_type=MESH
        )
    for r in range(1, 16):
        pl.semaphore_signal(barrier, 1, device_id={"seq": server(r)}, device_id_type=MESH)

    loads = []

    def load(src, dst):
        loads.append(pltpu.make_async_copy(src, dst, load_sem.at[len(loads)]))
        loads[-1].start()

    mine = grp.at[pl.ds(member * 4, 4)]
    first = [
        pltpu.make_async_copy(reads_hbm, reads, load_sem.at[9]),
        pltpu.make_async_copy(pkeys, mine.at[:, :, :, pl.ds(0, HD)], load_sem.at[10]),
        pltpu.make_async_copy(pvalues, mine.at[:, :, :, pl.ds(HD, HD)], load_sem.at[11]),
    ]
    for c in first:
        c.start()
    load(hid, hs)
    load(queries, qv)
    load(key_w.at[pl.ds(tp * FEAT, FEAT)], wkv.at[0, :, pl.ds(0, HD)])
    load(value_w.at[pl.ds(tp * FEAT, FEAT)], wkv.at[0, :, pl.ds(HD, HD)])
    load(og, gs.at[3])
    for j in range(TP):
        load(out_w.at[:, pl.ds(j * FEAT, FEAT)], wo.at[j])

    for c in first:
        c.wait()

    pl.semaphore_wait(barrier, 21)

    def ring(src, dst, k):
        lo, hi = pl.ds(0, HALF), pl.ds(HALF, HALF)

        def copy(s, d, n, to):
            return pltpu.make_async_remote_copy(
                s, d, ys_sem.at[k + n], yr_sem.at[k + n],
                device_id={"tp": to}, device_id_type=MESH,
            )

        own = [
            copy(src.at[lo], dst.at[0, lo], 0, right),
            copy(src.at[hi], dst.at[1, hi], 1, left),
            copy(src.at[hi], dst.at[0, hi], 2, right),
            copy(src.at[lo], dst.at[1, lo], 3, left),
        ]
        forward = [
            copy(dst.at[0, lo], dst.at[2, lo], 4, right),
            copy(dst.at[1, hi], dst.at[2, hi], 5, left),
        ]
        return own, forward

    piece = pl.ds((core * NX + xpos) * PIECE, PIECE)
    w_far = []
    for d in (2, 1, 3):
        to = (tp + d) % TP
        rows = pl.ds(to * FEAT + (core * NX + xpos) * PIECE, PIECE)
        for n, src in enumerate((key_w, value_w)):
            c = pltpu.make_async_remote_copy(
                src.at[rows], wkv.at[TP - d, piece, pl.ds(n * HD, HD)],
                wy_send.at[d, n], wy_recv.at[d, n], device_id={"tp": to}, device_id_type=MESH,
            )
            c.start()
            w_far.append(c)
    o_own, o_fwd = ring(og, gs, 0)
    for c in o_own:
        c.start()

    group = []
    for p in (3, 2, 1):
        c = pltpu.make_async_remote_copy(
            mine, mine,
            g_send.at[p], g_recv.at[p],
            device_id={"seq": level * 4 + peer(p)}, device_id_type=MESH,
        )
        c.start()
        group.append(c)

    rd = [lax.bitwise_and(reads[level, reader(r)], 15) for r in range(16)]
    lane = lax.broadcasted_iota(jnp.int32, (PBLK, TOK), 1)
    sub = lax.broadcasted_iota(jnp.int32, (PBLK, TOK), 0)
    want = lane % QROWS
    for r in range(16):
        want = want + jnp.where(lane // QROWS == r, rd[r] * QROWS, 0)
    for p in range(4):
        match = (sub + peer(p) * PBLK) == want
        hot[p * PBLK : (p + 1) * PBLK, :] = jnp.where(match, 1.0, 0.0).astype(BF)

    loads[1].wait()
    for h in range(HEADS):
        qt[h] = qv[:, h * HD : (h + 1) * HD].T

    for c in w_far:
        c.wait_recv()
    mate = {"seq": level * 4 + peer(1)}

    def pass_on(src_x, sems, n, to):
        rows = pl.ds((core * NX + src_x) * PIECE, PIECE)
        part = wkv.at[pl.ds(1, TP - 1), rows]
        return pltpu.make_async_remote_copy(
            part, part, sems[0].at[n], sems[1].at[n], device_id=to, device_id_type=MESH
        )

    w_row = []
    for i in (2, 1, 3):
        w_row.append(
            pass_on(xpos, (wx_send, wx_recv), i, {"seq": seq_of((xpos + i) % NX, zpos)})
        )
        w_row[-1].start()
    w_mate = [pass_on(xpos, (wc_send, wc_recv), 0, mate)]
    w_mate[0].start()

    for c in group:
        c.wait_recv()
    serve = [None]
    for q in range(QUART):
        kv[q, 0] = grp[rd[0], q]
    for r in range(1, 16):
        snd[r] = grp[rd[r]]
        c = pltpu.make_async_remote_copy(
            snd.at[r], kv.at[pl.ds(0, QUART), r], a_send.at[r], a_recv.at[r],
            device_id={"seq": reader(r)}, device_id_type=MESH,
        )
        c.start()
        serve.append(c)

    o_own[0].wait_recv()
    o_fwd[0].start()
    o_own[1].wait_recv()
    o_fwd[1].start()

    for i, c in zip((2, 1, 3), w_row):
        c.wait_recv()
        w_mate.append(pass_on((xpos + NX - i) % NX, (wc_send, wc_recv), i, mate))
        w_mate[-1].start()

    for n in range(4, 9):
        loads[n].wait()
    cgacc[...] = dot_nt(wo[tp], gs[3])
    o_own[2].wait_recv()
    cgacc[...] += dot_nt(wo[left], gs[0])
    o_own[3].wait_recv()
    cgacc[...] += dot_nt(wo[right], gs[1])

    for n in (0, 2, 3):
        loads[n].wait()
    for c in w_mate:
        c.wait_recv()
    new_far = []
    for d in (2, 1, 3):
        kvs[d] = dot(hs[...], wkv[d]).astype(BF)
        c = pltpu.make_async_remote_copy(
            kvs.at[d], kvr.at[d], kv_send.at[d], kv_recv.at[d],
            device_id={"tp": (tp + d) % TP}, device_id_type=MESH,
        )
        c.start()
        new_far.append(c)
    new_own[...] = dot(hs[...], wkv[0])

    o_fwd[0].wait_recv()
    o_fwd[1].wait_recv()
    cgacc[...] += dot_nt(wo[across], gs[2])

    for r in range(1, 16):
        serve[r].wait_recv()
    for c in range(QUART):
        vt[:, c * TOK : (c + 1) * TOK] = kv[c, :, :, HD:].reshape(TOK, HD).T

    def forward(h):
        q_h = qt[h]
        peak = None
        for c in range(QUART):
            s = dot(kv[c, :, :, 0:HD].reshape(TOK, HD), q_h)
            st[h, c] = s
            top = jnp.max(s, axis=0, keepdims=True)
            peak = top if peak is None else jnp.maximum(peak, top)
        low = None
        for c in range(QUART):
            e = jnp.exp2((st[h, c] - peak) * (SCALE * LOG2E))
            part = jnp.sum(e, axis=0, keepdims=True)
            low = part if low is None else low + part
            es[h, c * TOK : (c + 1) * TOK, :] = e.astype(BF)
        peaks[h] = jnp.broadcast_to(peak, (8, TOK))
        lows[h] = jnp.broadcast_to(low, (8, TOK))
        ctxt[h] = dot(vt[...], es[h])

    for h in range(HEADS):
        forward(h)
    for c in new_far:
        c.wait_recv()
    total = new_own[...]
    for d in (1, 2, 3):
        total += kvr[d].astype(F32)
    total = total.astype(BF)
    own_k[...] = total[:, 0:HD]
    own_vt[...] = total[:, HD:].T
    key_pos = lax.broadcasted_iota(jnp.int32, (TOK, TOK), 0)
    tok_pos = lax.broadcasted_iota(jnp.int32, (TOK, TOK), 1)
    visible = key_pos <= tok_pos
    for h in range(HEADS):
        s = jnp.where(visible, dot(own_k[...], qt[h]), -jnp.inf)
        old = peaks[h, 0:1, :]
        peak = jnp.maximum(jnp.max(s, axis=0, keepdims=True), old)
        e = jnp.exp2((s - peak) * (SCALE * LOG2E))
        shrink = jnp.exp2((old - peak) * (SCALE * LOG2E))
        low = lows[h, 0:1, :] * shrink + jnp.sum(e, axis=0, keepdims=True)
        scale = 1.0 / low
        gain = shrink * scale
        inv[h] = jnp.broadcast_to(gain, (8, TOK))
        joined = ctxt[h] * gain + dot(own_vt[...], e.astype(BF)) * scale
        ctxt[h] = joined
        ctx[:, h * HD : (h + 1) * HD] = joined.astype(BF).T

    def rs(src, dst, n, to):
        return pltpu.make_async_remote_copy(
            src, dst, r_send.at[n], r_recv.at[n], device_id={"tp": to}, device_id_type=MESH
        )

    lo, hi = pl.ds(0, HALF), pl.ds(HALF, HALF)
    rs_far = [
        rs(rs_fwd.at[lo], rs_mid.at[0], 0, right),
        rs(rs_fwd.at[hi], rs_mid.at[1], 1, left),
    ]
    rs_now = [
        rs(rs_own.at[0, hi], rs_in.at[0, hi], 2, right),
        rs(rs_own.at[1, lo], rs_in.at[1, lo], 3, left),
    ]
    rs_late = [
        rs(rs_own.at[0, lo], rs_in.at[0, lo], 4, right),
        rs(rs_own.at[1, hi], rs_in.at[1, hi], 5, left),
    ]
    rs_fwd[...] = dot(ctx[...], wo[across]).astype(BF)
    for c in rs_far:
        c.start()
    for h in range(HEADS):
        scaled = (cgacc[h * HD : (h + 1) * HD, :] * inv[h, 0:1, :]).astype(BF)
        cgt[h] = scaled
        cgn[h] = scaled.T
        delta = jnp.sum(scaled.astype(F32) * ctxt[h], axis=0, keepdims=True)
        inv[h] = jnp.broadcast_to(delta, (8, TOK))

    back = []

    def backward(i):
        rows = slice(i * TOK, (i + 1) * TOK)
        vals = kv[i, :, :, HD:].reshape(TOK, HD)
        dk = None
        for h in range(HEADS):
            slope = dot(vals, cgt[h])
            e = es[h, rows, :]
            grad = (e.astype(F32) * (slope - inv[h, 0:1, :])).astype(BF)
            dk_h = dot(grad, qv[:, h * HD : (h + 1) * HD])
            dv_h = dot(e, cgn[h])
            dk = dk_h if dk is None else dk + dk_h
            dv = dv_h if h == 0 else dv + dv_h
        gsend[i, :, :, 0:HD] = dk.astype(BF).reshape(16, QROWS, HD)
        gsend[i, :, :, HD:] = dv.astype(BF).reshape(16, QROWS, HD)
        grecv[i, 0] = gsend[i, 0]
        copies = []
        for r in FAR_FIRST:
            c = pltpu.make_async_remote_copy(
                gsend.at[i, r], grecv.at[i, r], b_send.at[i, r], b_recv.at[i, r],
                device_id={"seq": server(r)}, device_id_type=MESH,
            )
            c.start()
            copies.append(c)
        back.append(copies)

    backward(0)
    rs_own[0] = dot(ctx[...], wo[right]).astype(BF)
    rs_own[1] = dot(ctx[...], wo[left]).astype(BF)
    for c in rs_now:
        c.start()
    backward(1)
    rs_far[0].wait_recv()
    rs_own[0, 0:HALF] = (rs_own[0, 0:HALF].astype(F32) + rs_mid[0].astype(F32)).astype(BF)
    rs_late[0].start()
    rs_far[1].wait_recv()
    rs_own[1, HALF:] = (rs_own[1, HALF:].astype(F32) + rs_mid[1].astype(F32)).astype(BF)
    rs_late[1].start()
    backward(2)
    backward(3)

    kept = dot(ctx[...], wo[tp])

    spread = []
    for i in range(QUART):
        for c in back[i]:
            c.wait_recv()
        part = dot(hot[...], grecv[i].reshape(TOK, 2 * HD))
        own_grad[i] = part[0:PBLK, :]
        for p in (3, 2, 1):
            psend[p, i] = part[p * PBLK : (p + 1) * PBLK, :].astype(BF)
            c = pltpu.make_async_remote_copy(
                psend.at[p, i], precv.at[p, i], p_send.at[p, i], p_recv.at[p, i],
                device_id={"seq": level * 4 + peer(p)}, device_id_type=MESH,
            )
            c.start()
            spread.append(c)

    for c in rs_now + rs_late:
        c.wait_recv()
    out[...] = (kept + rs_in[0].astype(F32) + rs_in[1].astype(F32)).astype(BF)

    for i in range(QUART):
        for c in spread[3 * i : 3 * i + 3]:
            c.wait_recv()
        total = own_grad[i]
        for p in (1, 2, 3):
            total = total + precv[p, i].astype(F32)
        grads[:, i, :, 0:HD] = (total[:, 0:HD] * SCALE).reshape(4, QROWS, HD)
        grads[:, i, :, HD:] = total[:, HD:].reshape(4, QROWS, HD)

    for c in w_far + w_row + w_mate + new_far + o_own + o_fwd + group + rs_far + rs_now + rs_late + spread:
        c.wait_send()
    for r in range(1, 16):
        serve[r].wait_send()
    for copies in back:
        for c in copies:
            c.wait_send()


def local(*args):
    hidden, queries, key_w, value_w, out_w, pkeys, pvalues, reads, og = args
    pkeys = pkeys.reshape(4, QUART, QROWS, HD)
    pvalues = pvalues.reshape(4, QUART, QROWS, HD)
    operands = (reads.T, hidden, queries, key_w, value_w, out_w, pkeys, pvalues, og)
    operands = [pltpu.with_memory_space_constraint(a, pltpu.HBM) for a in operands]
    vmem = pl.BlockSpec(memory_space=pltpu.VMEM)
    hbm = pl.BlockSpec(memory_space=pltpu.HBM)
    dma = pltpu.SemaphoreType.DMA
    V = pltpu.VMEM
    out, grads = pl.pallas_call(
        kernel,
        out_shape=(
            jax.ShapeDtypeStruct((TOK, FEAT), BF),
            jax.ShapeDtypeStruct((4, QUART, QROWS, 2 * HD), F32),
        ),
        in_specs=[hbm] * 9,
        out_specs=(vmem, vmem),
        scratch_shapes=[
            pltpu.SMEM((16, 64), jnp.int32),
            V((TOK, FEAT), BF),
            V((4, TOK, FEAT), BF),
            V((TP, FEAT, 2 * HD), BF),
            V((TP, FEAT, FEAT), BF),
            V((TOK, FEAT), BF),
            V((HEADS, HD, TOK), BF),
            V((16, QUART, QROWS, 2 * HD), BF),
            V((16, QUART, QROWS, 2 * HD), BF),
            V((QUART, 16, QROWS, 2 * HD), BF),
            V((HD, KEYS), BF),
            V((TOK, TOK), BF),
            V((HEADS, QUART, TOK, TOK), F32),
            V((HEADS, KEYS, TOK), BF),
            V((HEADS, 8, TOK), F32),
            V((HEADS, 8, TOK), F32),
            V((TOK, HD), BF),
            V((HD, TOK), BF),
            V((TOK, 2 * HD), F32),
            V((HEADS, HD, TOK), F32),
            V((TOK, FEAT), BF),
            V((HEADS, 8, TOK), F32),
            V((FEAT, TOK), F32),
            V((TP, TOK, 2 * HD), BF),
            V((TP, TOK, 2 * HD), BF),
            V((HEADS, HD, TOK), BF),
            V((HEADS, TOK, HD), BF),
            V((QUART, 16, QROWS, 2 * HD), BF),
            V((QUART, 16, QROWS, 2 * HD), BF),
            V((4, QUART, PBLK, 2 * HD), BF),
            V((4, QUART, PBLK, 2 * HD), BF),
            V((QUART, PBLK, 2 * HD), F32),
            V((2, TOK, FEAT), BF),
            V((TOK, FEAT), BF),
            V((2, HALF, FEAT), BF),
            V((2, TOK, FEAT), BF),
            dma((12,)), dma((6,)), dma((6,)), dma((4,)), dma((4,)), dma((16,)), dma((16,)),
            dma((QUART, 16)), dma((QUART, 16)), dma((4, QUART)), dma((4, QUART)), dma((6,)), dma((6,)),
            dma((4, 2)), dma((4, 2)), dma((4,)), dma((4,)), dma((4,)), dma((4,)), dma((4,)), dma((4,)),
        ],
        compiler_params=pltpu.CompilerParams(
            collective_id=0, has_side_effects=True, vmem_limit_bytes=40 * 1024 * 1024
        ),
    )(*operands)
    grads = grads.reshape(TOK, 2 * HD)
    return out, grads[:, 0:HD], grads[:, HD:]


def solution(mesh):
    in_specs = (
        P("seq", "tp"), P("seq", "tp"), P(None, "tp"), P(None, "tp"), P("tp", None),
        P("seq", "tp"), P("seq", "tp"), P(), P("seq", "tp"),
    )
    out_specs = (P("seq", "tp"), P("seq", "tp"), P("seq", "tp"))
    return jax.shard_map(local, mesh=mesh, in_specs=in_specs, out_specs=out_specs, check_vma=False)
```

```python
import functools

import jax
import jax.numpy as jnp
from jax import lax
from jax.experimental import pallas as pl
from jax.experimental.pallas import tpu as pltpu
from jax.sharding import PartitionSpec as P

HD = 128
PBLK = 64
NX, NZ = 4, 8
TP = 4
HEADS = 7
TOK = 256
KEYS = 1024
FEAT = 896
HALF = TOK // 2
QUART = 4
QROWS = PBLK // QUART
PIECE = FEAT // (2 * NX)
SCALE = HD ** -0.5
LOG2E = 1.4426950408889634
BF = jnp.bfloat16
F32 = jnp.float32
MESH = pl.DeviceIdType.MESH
FAR_FIRST = (11, 10, 7, 15, 9, 8, 6, 14, 3, 2, 5, 13, 1, 4, 12)


def dot(a, b):
    return jnp.dot(a, b, preferred_element_type=F32)


def dot_nt(a, b):
    return lax.dot_general(a, b, (((1,), (1,)), ((), ())), preferred_element_type=F32)


def kernel(
    reads_hbm, hid, queries, key_w, value_w, out_w, pkeys, pvalues, og,
    out, grads,
    reads, hs, gs, wkv, wo, qv, qt, grp, snd, kv, vt, hot, st, es, peaks, lows, own_k, own_vt, new_own, ctxt, ctx, inv, cgacc, kvs, kvr, cgt,
    gsend, grecv, psend, precv, own_grad, rs_own, rs_fwd, rs_mid, rs_in,
    load_sem, ys_sem, yr_sem, g_send, g_recv, a_send, a_recv, b_send, b_recv, p_send, p_recv,
    r_send, r_recv, wy_send, wy_recv, wx_send, wx_recv, wc_send, wc_recv, kv_send, kv_recv,
):
    seq = lax.axis_index("seq")
    tp = lax.axis_index("tp")
    core = seq % 2
    zpos = (seq // 2) % NZ
    xpos = seq // (2 * NZ)
    member = seq % 4
    level = seq // 4
    right = (tp + 1) % TP
    left = (tp + TP - 1) % TP
    across = (tp + 2) % TP
    step = 2 * (zpos % 2) - 1

    def seq_of(x, z):
        return (x * NZ + z) * 2 + core

    def reader(r):
        i, j = r // 4, r % 4
        return seq_of((xpos + i) % NX, (zpos + step * j + NZ) % NZ)

    def server(r):
        i, j = r // 4, r % 4
        even = (zpos + j) % 2
        z = (zpos + j - 2 * j * even + NZ) % NZ
        return seq_of((xpos + NX - i) % NX, z)

    def peer(p):
        low = member
        bit0, bit1 = low % 2, low // 2
        if p % 2:
            bit0 = 1 - bit0
        if p // 2:
            bit1 = 1 - bit1
        return bit1 * 2 + bit0

    barrier = pltpu.get_barrier_semaphore()
    for t in (left, right, across):
        pl.semaphore_signal(barrier, 1, device_id={"tp": t}, device_id_type=MESH)
    for p in (1, 2, 3):
        pl.semaphore_signal(
            barrier, 1, device_id={"seq": level * 4 + peer(p)}, device_id_type=MESH
        )
    for r in range(1, 16):
        pl.semaphore_signal(barrier, 1, device_id={"seq": server(r)}, device_id_type=MESH)

    loads = []

    def load(src, dst):
        loads.append(pltpu.make_async_copy(src, dst, load_sem.at[len(loads)]))
        loads[-1].start()

    mine = grp.at[pl.ds(member * 4, 4)]
    first = [
        pltpu.make_async_copy(reads_hbm, reads, load_sem.at[9]),
        pltpu.make_async_copy(pkeys, mine.at[:, :, :, pl.ds(0, HD)], load_sem.at[10]),
        pltpu.make_async_copy(pvalues, mine.at[:, :, :, pl.ds(HD, HD)], load_sem.at[11]),
    ]
    for c in first:
        c.start()
    load(hid, hs)
    load(queries, qv)
    load(key_w.at[pl.ds(tp * FEAT, FEAT)], wkv.at[0, :, pl.ds(0, HD)])
    load(value_w.at[pl.ds(tp * FEAT, FEAT)], wkv.at[0, :, pl.ds(HD, HD)])
    load(og, gs.at[3])
    for j in range(TP):
        load(out_w.at[:, pl.ds(j * FEAT, FEAT)], wo.at[j])

    for c in first:
        c.wait()

    pl.semaphore_wait(barrier, 21)

    def ring(src, dst, k):
        lo, hi = pl.ds(0, HALF), pl.ds(HALF, HALF)

        def copy(s, d, n, to):
            return pltpu.make_async_remote_copy(
                s, d, ys_sem.at[k + n], yr_sem.at[k + n],
                device_id={"tp": to}, device_id_type=MESH,
            )

        own = [
            copy(src.at[lo], dst.at[0, lo], 0, right),
            copy(src.at[hi], dst.at[1, hi], 1, left),
            copy(src.at[hi], dst.at[0, hi], 2, right),
            copy(src.at[lo], dst.at[1, lo], 3, left),
        ]
        forward = [
            copy(dst.at[0, lo], dst.at[2, lo], 4, right),
            copy(dst.at[1, hi], dst.at[2, hi], 5, left),
        ]
        return own, forward

    piece = pl.ds((core * NX + xpos) * PIECE, PIECE)
    w_far = []
    for d in (2, 1, 3):
        to = (tp + d) % TP
        rows = pl.ds(to * FEAT + (core * NX + xpos) * PIECE, PIECE)
        for n, src in enumerate((key_w, value_w)):
            c = pltpu.make_async_remote_copy(
                src.at[rows], wkv.at[TP - d, piece, pl.ds(n * HD, HD)],
                wy_send.at[d, n], wy_recv.at[d, n], device_id={"tp": to}, device_id_type=MESH,
            )
            c.start()
            w_far.append(c)
    o_own, o_fwd = ring(og, gs, 0)
    for c in o_own:
        c.start()

    group = []
    for p in (3, 2, 1):
        c = pltpu.make_async_remote_copy(
            mine, mine,
            g_send.at[p], g_recv.at[p],
            device_id={"seq": level * 4 + peer(p)}, device_id_type=MESH,
        )
        c.start()
        group.append(c)

    rd = [lax.bitwise_and(reads[level, reader(r)], 15) for r in range(16)]
    lane = lax.broadcasted_iota(jnp.int32, (PBLK, TOK), 1)
    sub = lax.broadcasted_iota(jnp.int32, (PBLK, TOK), 0)
    want = lane % QROWS
    for r in range(16):
        want = want + jnp.where(lane // QROWS == r, rd[r] * QROWS, 0)
    for p in range(4):
        match = (sub + peer(p) * PBLK) == want
        hot[p * PBLK : (p + 1) * PBLK, :] = jnp.where(match, 1.0, 0.0).astype(BF)

    loads[1].wait()
    for h in range(HEADS):
        qt[h] = qv[:, h * HD : (h + 1) * HD].T

    for c in w_far:
        c.wait_recv()
    mate = {"seq": level * 4 + peer(1)}

    def pass_on(src_x, sems, n, to):
        rows = pl.ds((core * NX + src_x) * PIECE, PIECE)
        part = wkv.at[pl.ds(1, TP - 1), rows]
        return pltpu.make_async_remote_copy(
            part, part, sems[0].at[n], sems[1].at[n], device_id=to, device_id_type=MESH
        )

    w_row = []
    for i in (2, 1, 3):
        w_row.append(
            pass_on(xpos, (wx_send, wx_recv), i, {"seq": seq_of((xpos + i) % NX, zpos)})
        )
        w_row[-1].start()
    w_mate = [pass_on(xpos, (wc_send, wc_recv), 0, mate)]
    w_mate[0].start()

    for c in group:
        c.wait_recv()
    serve = [None]
    for q in range(QUART):
        kv[q, 0] = grp[rd[0], q]
    for r in range(1, 16):
        snd[r] = grp[rd[r]]
        c = pltpu.make_async_remote_copy(
            snd.at[r], kv.at[pl.ds(0, QUART), r], a_send.at[r], a_recv.at[r],
            device_id={"seq": reader(r)}, device_id_type=MESH,
        )
        c.start()
        serve.append(c)

    o_own[0].wait_recv()
    o_fwd[0].start()
    o_own[1].wait_recv()
    o_fwd[1].start()

    for i, c in zip((2, 1, 3), w_row):
        c.wait_recv()
        w_mate.append(pass_on((xpos + NX - i) % NX, (wc_send, wc_recv), i, mate))
        w_mate[-1].start()

    for n in range(4, 9):
        loads[n].wait()
    cgacc[...] = dot_nt(wo[tp], gs[3])
    o_own[2].wait_recv()
    cgacc[...] += dot_nt(wo[left], gs[0])
    o_own[3].wait_recv()
    cgacc[...] += dot_nt(wo[right], gs[1])

    for n in (0, 2, 3):
        loads[n].wait()
    for c in w_mate:
        c.wait_recv()
    new_far = []
    for d in (2, 1, 3):
        kvs[d] = dot(hs[...], wkv[d]).astype(BF)
        c = pltpu.make_async_remote_copy(
            kvs.at[d], kvr.at[d], kv_send.at[d], kv_recv.at[d],
            device_id={"tp": (tp + d) % TP}, device_id_type=MESH,
        )
        c.start()
        new_far.append(c)
    new_own[...] = dot(hs[...], wkv[0])

    o_fwd[0].wait_recv()
    o_fwd[1].wait_recv()
    cgacc[...] += dot_nt(wo[across], gs[2])

    for r in range(1, 16):
        serve[r].wait_recv()
    for c in range(QUART):
        vt[:, c * TOK : (c + 1) * TOK] = kv[c, :, :, HD:].reshape(TOK, HD).T

    def forward(h):
        q_h = qt[h]
        peak = None
        for c in range(QUART):
            s = dot(kv[c, :, :, 0:HD].reshape(TOK, HD), q_h)
            st[h, c] = s
            top = jnp.max(s, axis=0, keepdims=True)
            peak = top if peak is None else jnp.maximum(peak, top)
        low = None
        for c in range(QUART):
            e = jnp.exp2((st[h, c] - peak) * (SCALE * LOG2E))
            part = jnp.sum(e, axis=0, keepdims=True)
            low = part if low is None else low + part
            es[h, c * TOK : (c + 1) * TOK, :] = e.astype(BF)
        peaks[h] = jnp.broadcast_to(peak, (8, TOK))
        lows[h] = jnp.broadcast_to(low, (8, TOK))
        ctxt[h] = dot(vt[...], es[h])

    for h in range(HEADS):
        forward(h)
    for c in new_far:
        c.wait_recv()
    total = new_own[...]
    for d in (1, 2, 3):
        total += kvr[d].astype(F32)
    total = total.astype(BF)
    own_k[...] = total[:, 0:HD]
    own_vt[...] = total[:, HD:].T
    key_pos = lax.broadcasted_iota(jnp.int32, (TOK, TOK), 0)
    tok_pos = lax.broadcasted_iota(jnp.int32, (TOK, TOK), 1)
    visible = key_pos <= tok_pos
    for h in range(HEADS):
        s = jnp.where(visible, dot(own_k[...], qt[h]), -jnp.inf)
        old = peaks[h, 0:1, :]
        peak = jnp.maximum(jnp.max(s, axis=0, keepdims=True), old)
        e = jnp.exp2((s - peak) * (SCALE * LOG2E))
        shrink = jnp.exp2((old - peak) * (SCALE * LOG2E))
        low = lows[h, 0:1, :] * shrink + jnp.sum(e, axis=0, keepdims=True)
        scale = 1.0 / low
        gain = shrink * scale
        inv[h] = jnp.broadcast_to(gain, (8, TOK))
        joined = ctxt[h] * gain + dot(own_vt[...], e.astype(BF)) * scale
        ctxt[h] = joined
        ctx[:, h * HD : (h + 1) * HD] = joined.astype(BF).T

    def rs(src, dst, n, to):
        return pltpu.make_async_remote_copy(
            src, dst, r_send.at[n], r_recv.at[n], device_id={"tp": to}, device_id_type=MESH
        )

    lo, hi = pl.ds(0, HALF), pl.ds(HALF, HALF)
    rs_far = [
        rs(rs_fwd.at[lo], rs_mid.at[0], 0, right),
        rs(rs_fwd.at[hi], rs_mid.at[1], 1, left),
    ]
    rs_now = [
        rs(rs_own.at[0, hi], rs_in.at[0, hi], 2, right),
        rs(rs_own.at[1, lo], rs_in.at[1, lo], 3, left),
    ]
    rs_late = [
        rs(rs_own.at[0, lo], rs_in.at[0, lo], 4, right),
        rs(rs_own.at[1, hi], rs_in.at[1, hi], 5, left),
    ]
    rs_fwd[...] = dot(ctx[...], wo[across]).astype(BF)
    for c in rs_far:
        c.start()
    for h in range(HEADS):
        scaled = (cgacc[h * HD : (h + 1) * HD, :] * inv[h, 0:1, :]).astype(BF)
        cgt[h] = scaled
        delta = jnp.sum(scaled.astype(F32) * ctxt[h], axis=0, keepdims=True)
        inv[h] = jnp.broadcast_to(delta, (8, TOK))

    back = []

    def backward(i):
        rows = slice(i * TOK, (i + 1) * TOK)
        vals = kv[i, :, :, HD:].reshape(TOK, HD)
        dk = None
        for h in range(HEADS):
            slope = dot(vals, cgt[h])
            e = es[h, rows, :]
            grad = (e.astype(F32) * (slope - inv[h, 0:1, :])).astype(BF)
            dk_h = dot(grad, qv[:, h * HD : (h + 1) * HD])
            dv_h = dot_nt(e, cgt[h])
            dk = dk_h if dk is None else dk + dk_h
            dv = dv_h if h == 0 else dv + dv_h
        gsend[i, :, :, 0:HD] = dk.astype(BF).reshape(16, QROWS, HD)
        gsend[i, :, :, HD:] = dv.astype(BF).reshape(16, QROWS, HD)
        grecv[i, 0] = gsend[i, 0]
        copies = []
        for r in FAR_FIRST:
            c = pltpu.make_async_remote_copy(
                gsend.at[i, r], grecv.at[i, r], b_send.at[i, r], b_recv.at[i, r],
                device_id={"seq": server(r)}, device_id_type=MESH,
            )
            c.start()
            copies.append(c)
        back.append(copies)

    backward(0)
    rs_own[0] = dot(ctx[...], wo[right]).astype(BF)
    rs_own[1] = dot(ctx[...], wo[left]).astype(BF)
    for c in rs_now:
        c.start()
    backward(1)
    rs_far[0].wait_recv()
    rs_own[0, 0:HALF] = (rs_own[0, 0:HALF].astype(F32) + rs_mid[0].astype(F32)).astype(BF)
    rs_late[0].start()
    rs_far[1].wait_recv()
    rs_own[1, HALF:] = (rs_own[1, HALF:].astype(F32) + rs_mid[1].astype(F32)).astype(BF)
    rs_late[1].start()
    backward(2)
    backward(3)

    kept = dot(ctx[...], wo[tp])

    spread = []
    for i in range(QUART):
        for c in back[i]:
            c.wait_recv()
        part = dot(hot[...], grecv[i].reshape(TOK, 2 * HD))
        own_grad[i] = part[0:PBLK, :]
        for p in (3, 2, 1):
            psend[p, i] = part[p * PBLK : (p + 1) * PBLK, :].astype(BF)
            c = pltpu.make_async_remote_copy(
                psend.at[p, i], precv.at[p, i], p_send.at[p, i], p_recv.at[p, i],
                device_id={"seq": level * 4 + peer(p)}, device_id_type=MESH,
            )
            c.start()
            spread.append(c)

    for c in rs_now + rs_late:
        c.wait_recv()
    out[...] = (kept + rs_in[0].astype(F32) + rs_in[1].astype(F32)).astype(BF)

    for i in range(QUART):
        for c in spread[3 * i : 3 * i + 3]:
            c.wait_recv()
        total = own_grad[i]
        for p in (1, 2, 3):
            total = total + precv[p, i].astype(F32)
        grads[:, i, :, 0:HD] = (total[:, 0:HD] * SCALE).reshape(4, QROWS, HD)
        grads[:, i, :, HD:] = total[:, HD:].reshape(4, QROWS, HD)

    for c in w_far + w_row + w_mate + new_far + o_own + o_fwd + group + rs_far + rs_now + rs_late + spread:
        c.wait_send()
    for r in range(1, 16):
        serve[r].wait_send()
    for copies in back:
        for c in copies:
            c.wait_send()


def local(*args):
    hidden, queries, key_w, value_w, out_w, pkeys, pvalues, reads, og = args
    pkeys = pkeys.reshape(4, QUART, QROWS, HD)
    pvalues = pvalues.reshape(4, QUART, QROWS, HD)
    operands = (reads.T, hidden, queries, key_w, value_w, out_w, pkeys, pvalues, og)
    operands = [pltpu.with_memory_space_constraint(a, pltpu.HBM) for a in operands]
    vmem = pl.BlockSpec(memory_space=pltpu.VMEM)
    hbm = pl.BlockSpec(memory_space=pltpu.HBM)
    dma = pltpu.SemaphoreType.DMA
    V = pltpu.VMEM
    out, grads = pl.pallas_call(
        kernel,
        out_shape=(
            jax.ShapeDtypeStruct((TOK, FEAT), BF),
            jax.ShapeDtypeStruct((4, QUART, QROWS, 2 * HD), F32),
        ),
        in_specs=[hbm] * 9,
        out_specs=(vmem, vmem),
        scratch_shapes=[
            pltpu.SMEM((16, 64), jnp.int32),
            V((TOK, FEAT), BF),
            V((4, TOK, FEAT), BF),
            V((TP, FEAT, 2 * HD), BF),
            V((TP, FEAT, FEAT), BF),
            V((TOK, FEAT), BF),
            V((HEADS, HD, TOK), BF),
            V((16, QUART, QROWS, 2 * HD), BF),
            V((16, QUART, QROWS, 2 * HD), BF),
            V((QUART, 16, QROWS, 2 * HD), BF),
            V((HD, KEYS), BF),
            V((TOK, TOK), BF),
            V((HEADS, QUART, TOK, TOK), F32),
            V((HEADS, KEYS, TOK), BF),
            V((HEADS, 8, TOK), F32),
            V((HEADS, 8, TOK), F32),
            V((TOK, HD), BF),
            V((HD, TOK), BF),
            V((TOK, 2 * HD), F32),
            V((HEADS, HD, TOK), F32),
            V((TOK, FEAT), BF),
            V((HEADS, 8, TOK), F32),
            V((FEAT, TOK), F32),
            V((TP, TOK, 2 * HD), BF),
            V((TP, TOK, 2 * HD), BF),
            V((HEADS, HD, TOK), BF),
            V((QUART, 16, QROWS, 2 * HD), BF),
            V((QUART, 16, QROWS, 2 * HD), BF),
            V((4, QUART, PBLK, 2 * HD), BF),
            V((4, QUART, PBLK, 2 * HD), BF),
            V((QUART, PBLK, 2 * HD), F32),
            V((2, TOK, FEAT), BF),
            V((TOK, FEAT), BF),
            V((2, HALF, FEAT), BF),
            V((2, TOK, FEAT), BF),
            dma((12,)), dma((6,)), dma((6,)), dma((4,)), dma((4,)), dma((16,)), dma((16,)),
            dma((QUART, 16)), dma((QUART, 16)), dma((4, QUART)), dma((4, QUART)), dma((6,)), dma((6,)),
            dma((4, 2)), dma((4, 2)), dma((4,)), dma((4,)), dma((4,)), dma((4,)), dma((4,)), dma((4,)),
        ],
        compiler_params=pltpu.CompilerParams(
            collective_id=0, has_side_effects=True, vmem_limit_bytes=40 * 1024 * 1024
        ),
    )(*operands)
    grads = grads.reshape(TOK, 2 * HD)
    return out, grads[:, 0:HD], grads[:, HD:]


def solution(mesh):
    in_specs = (
        P("seq", "tp"), P("seq", "tp"), P(None, "tp"), P(None, "tp"), P("tp", None),
        P("seq", "tp"), P("seq", "tp"), P(), P("seq", "tp"),
    )
    out_specs = (P("seq", "tp"), P("seq", "tp"), P("seq", "tp"))
    return jax.shard_map(local, mesh=mesh, in_specs=in_specs, out_specs=out_specs, check_vma=False)
```
